32 devices in a mesh: ctx: 16 (over z, y, core), tp: 2 (over x).
Axes of the slice: x: 2, y: 2, z: 4, core: 2. Of those that a mesh axis runs over, the one named last changes fastest.
Arguments:
- queries: bfloat16 [1024, 1536], P('ctx', 'tp'), may hold values from -512 to 512
- keys: bfloat16 [1024, 1536], P('ctx', 'tp'), may hold values from -8 to 8
- values: bfloat16 [1024, 1536], P('ctx', 'tp'), may hold values from -6 to 6
- wo: bfloat16 [1536, 3072], P('tp'), may hold values from -0.15625 to 0.15625
- frame_tokens: int32 [16], replicated, may hold values from 32 to 64, as said below
Outputs:
- projected: bfloat16 [1024, 3072], P(('ctx', 'tp'))
The draws below stay inside these ranges and needn't reach their ends.
Inputs may be any that keep to these rules, and one draw needn't show every extreme that they name: `frame_tokens`: at least 32 tokens of every frame are live.
All inputs are finite; a program needn't handle non-finite values.
Results may differ from the reference program's by a relative error of at most 0.014.
Values may be sent and summed in bfloat16 or wider, within the bound.
A program may use at most 128 MiB of HBM per device.

```python
import math
import jax
import jax.numpy as jnp
from jax import lax

WIDTH = 3072
HEADS = 12
HEAD_DIM = 128
FRAME = 64
FRAMES = 16
TOKENS = 1024


def shared_fields(key):
    columns = HEADS * HEAD_DIM
    key_drawn = jnp.clip(jax.random.normal(jax.random.fold_in(key, 11), (TOKENS, columns), jnp.float32), -6.0, 6.0)
    query_drawn = jnp.clip(2.5 * jax.random.normal(jax.random.fold_in(key, 12), (TOKENS, columns), jnp.float32), -15.0, 15.0)
    return (key_drawn, query_drawn)


def draw_queries(key, part):
    key_field, query_field = shared_fields(key)
    return query_field.astype(jnp.bfloat16)


def draw_keys(key, part):
    key_field, query_field = shared_fields(key)
    return key_field.astype(jnp.bfloat16)


def draw_frame_tokens(key, part):
    counts = jax.random.randint(jax.random.fold_in(key, 21), (FRAMES,), FRAME // 2, FRAME + 1)
    fullest = jax.random.randint(jax.random.fold_in(key, 22), (), 0, FRAMES)
    emptiest = jax.random.randint(jax.random.fold_in(key, 23), (), 0, FRAMES)
    frame_ids = jnp.arange(FRAMES, dtype=jnp.int32)
    counts = jnp.where(frame_ids == emptiest, FRAME // 2, counts)
    counts = jnp.where(frame_ids == fullest, FRAME, counts)
    return counts.astype(jnp.int32)


def shard_levels(own_key, dims, cuts, smallest, high):
    level, own = 1.0, jax.random.fold_in(own_key, 6)
    for dim, shards_of in cuts:
        steps = jnp.exp(jax.random.uniform(jax.random.fold_in(own, dim), (shards_of,), jnp.float32, smallest / len(cuts), high / len(cuts)))
        level = level * jnp.repeat(steps, dims[dim] // shards_of).reshape([-1 if axis == dim else 1 for axis in range(len(dims))])
    return level


def normal_values(rng, extent, deviation, bound, cuts=(), kind=jnp.bfloat16):
    gain = shard_levels(rng, extent, cuts, -0.22, 0.18) if cuts else 1.0
    values = jax.random.normal(rng, extent, jnp.float32) * deviation * gain
    return jnp.minimum(jnp.maximum(values, -bound), bound).astype(kind)


def setup_inputs(seed: int = 0) -> dict:
    arg_keys = jax.random.split(jax.random.key(seed), 6)
    queries = draw_queries(jax.random.fold_in(arg_keys[5], 71), 0)
    keys = draw_keys(jax.random.fold_in(arg_keys[5], 71), 0)
    values = normal_values(arg_keys[2], (TOKENS, HEADS * HEAD_DIM), 1.0, 6.0, ((0, 16), (1, 2)))
    wo = normal_values(arg_keys[3], (HEADS * HEAD_DIM, WIDTH), (HEADS * HEAD_DIM) ** -0.5, 0.15625, ((0, 2),))
    frame_tokens = draw_frame_tokens(jax.random.fold_in(arg_keys[5], 71), 0)
    return {"queries": queries, "keys": keys, "values": values, "wo": wo, "frame_tokens": frame_tokens}


def reference(queries, keys, values, wo, frame_tokens):
    total_rows = queries.shape[0]
    positions = jnp.arange(total_rows, dtype=jnp.int32)
    frame_index = positions // FRAME
    live_mask = positions % FRAME < frame_tokens[frame_index]
    query_all = queries.astype(jnp.float32).reshape(total_rows, HEADS, HEAD_DIM)
    key_all = keys.astype(jnp.float32).reshape(total_rows, HEADS, HEAD_DIM)
    value_all = values.astype(jnp.float32).reshape(total_rows, HEADS, HEAD_DIM)
    block_rows = 512 if total_rows % 512 == 0 else total_rows
    scale_factor = 1.0 / math.sqrt(HEAD_DIM)

    def one_block(start):
        query_block = lax.dynamic_slice_in_dim(query_all, start, block_rows, 0)
        frame_block = lax.dynamic_slice_in_dim(frame_index, start, block_rows, 0)
        live_block = lax.dynamic_slice_in_dim(live_mask, start, block_rows, 0)
        scores = jnp.einsum('qhd,khd->hqk', query_block, key_all) * scale_factor
        allowed = (frame_index[None, :] <= frame_block[:, None]) & live_mask[None, :]
        scores = jnp.where(allowed[None], scores, -jnp.inf)
        row_max = lax.optimization_barrier(jnp.max(scores, axis=-1, keepdims=True))
        weights = jnp.exp(scores - row_max)
        totals = lax.optimization_barrier(jnp.sum(weights, axis=-1))
        rounded = lax.optimization_barrier(weights.astype(jnp.bfloat16)).astype(jnp.float32)
        summed = jnp.einsum('hqk,khd->qhd', rounded, value_all)
        heads_out = summed / jnp.transpose(totals)[:, :, None]
        heads_out = jnp.where(live_block[:, None, None], heads_out, 0.0)
        return heads_out.astype(jnp.bfloat16)
    block_starts = jnp.arange(0, total_rows, block_rows, dtype=jnp.int32)
    blocks_out = lax.map(one_block, block_starts)
    attended = blocks_out.reshape(total_rows, HEADS * HEAD_DIM)
    return jnp.dot(attended, wo, preferred_element_type=jnp.float32).astype(jnp.bfloat16)
```

```python
import functools
import math

import jax
import jax.numpy as jnp
from jax import lax
from jax.experimental import pallas as pl
from jax.experimental.pallas import tpu as pltpu
from jax.sharding import PartitionSpec as P

HEAD_DIM = 128
LAYER = 4
BLOCKS = 2
NEG = -1e30
MESH = pl.DeviceIdType.MESH
FAR, NEAR = 0, 1


def group_size(n):
    levels = n // LAYER
    return n // 2 if levels % 2 == 0 else n


def host_offsets(size, head_count):
    top = size // LAYER - 1
    places = []
    for h in range(head_count):
        spread = h % LAYER
        places.append((top - h // LAYER) * LAYER + (spread % 2) * (LAYER // 2) + spread // 2)
    return places


def kernel(
    n,
    chunk,
    counts_ref,
    q_hbm,
    k_hbm,
    v_hbm,
    wo_hbm,
    out_ref,
    q_ref,
    k_ref,
    v_ref,
    wo_all,
    k_in,
    v_in,
    q_in,
    acc_out,
    stat_out,
    acc_in,
    stat_in,
    stat_rows,
    attended,
    kept,
    outgoing,
    incoming,
    in_sem,
    wo_sem,
    k_send,
    v_send,
    q_send,
    far_send,
    k_recv,
    v_recv,
    q_recv,
    far_recv,
    acc_send,
    acc_recv,
    stat_send,
    stat_recv,
    x_send_sem,
    x_recv_sem,
):
    tok_rows, columns = k_hbm.shape
    head_count = columns // HEAD_DIM
    width = wo_hbm.shape[1]
    half = tok_rows // 2
    blocks = q_ref.shape[0]
    rb = q_ref.shape[1]
    sent_blocks = blocks // 2
    me = lax.axis_index("ctx")
    tp = lax.axis_index("tp")
    size = group_size(n)
    split = size < n
    upper = me // size
    base = upper * size
    local = me - base
    is_upper = upper > 0
    places = host_offsets(size, head_count)
    my_head = jnp.int32(0)
    is_host = local < 0
    for h, place in enumerate(places):
        my_head = jnp.where(local == place, h, my_head)
        is_host = jnp.logical_or(is_host, local == place)
    my_cols = pl.ds(pl.multiple_of(my_head * HEAD_DIM, HEAD_DIM), HEAD_DIM)
    head_cols = [slice(h * HEAD_DIM, (h + 1) * HEAD_DIM) for h in range(head_count)]
    scale = math.log2(math.e) / math.sqrt(HEAD_DIM)

    def start_of(b):
        side = (1 - tp) if b < sent_blocks else tp
        return pl.multiple_of(side * half + (b % sent_blocks) * rb, rb)

    def rows_of(src, rows):
        return pl.ds(pl.multiple_of(src * rows, rows), rows)

    loads = [
        pltpu.make_async_copy(k_hbm, k_ref, in_sem.at[0]),
        pltpu.make_async_copy(v_hbm, v_ref, in_sem.at[1]),
    ] + [
        pltpu.make_async_copy(q_hbm.at[pl.ds(start_of(b), rb), :], q_ref.at[b], in_sem.at[2 + b])
        for b in range(blocks)
    ]
    for load in loads:
        load.start()

    barrier = pltpu.get_barrier_semaphore()

    def greet(dev, other_tp):
        pl.semaphore_signal(barrier, inc=1, device_id=(dev, other_tp), device_id_type=MESH)

    def each(count, body):
        if count <= 16:
            for j in range(count):
                body(j)
        else:
            lax.fori_loop(0, count, lambda j, carry: (body(j), carry)[1], 0)

    greet(me, 1 - tp)

    @pl.when(is_host)
    def _():
        def other(j):
            @pl.when(local != j)
            def _():
                greet(base + j, tp)

        each(size, other)

    @pl.when(jnp.logical_not(is_host))
    def _():
        for place in places:
            greet(base + place, tp)

    expected = 1 + jnp.where(is_host, size - 1, head_count)
    if split:

        @pl.when(is_upper)
        def _():
            for place in places:
                greet(place, tp)

        @pl.when(jnp.logical_and(is_host, jnp.logical_not(is_upper)))
        def _():
            each(size, lambda j: greet(size + j, tp))

        expected = expected + jnp.where(is_upper, head_count, jnp.where(is_host, size, 0))
    with jax.named_scope("bar"):
        pl.semaphore_wait(barrier, expected)

    wo_copy = pltpu.make_async_copy(wo_hbm, wo_all, wo_sem)

    def remote(src, dst, send, recv, dev):
        return pltpu.make_async_remote_copy(
            src_ref=src,
            dst_ref=dst,
            send_sem=send,
            recv_sem=recv,
            device_id=(dev, tp),
            device_id_type=MESH,
        )

    def give_k(h, frame, dev):
        return remote(
            k_ref.at[:, head_cols[h]], k_in.at[rows_of(frame, tok_rows)], k_send.at[h], k_recv.at[frame], dev
        )

    def give_v(h, frame, dev):
        return remote(
            v_ref.at[:, head_cols[h]], v_in.at[rows_of(frame, tok_rows)], v_send.at[h], v_recv.at[frame], dev
        )

    def give_q(h, frame, dev):
        return remote(
            q_ref.at[:, :, head_cols[h]], q_in.at[NEAR, :, rows_of(frame, rb)], q_send.at[h], q_recv.at[frame], dev
        )

    def give_far(h, b, frame):
        return remote(
            q_ref.at[b, :, head_cols[h]],
            q_in.at[FAR, b, rows_of(frame, rb)],
            far_send.at[b, h],
            far_recv.at[b, frame],
            places[h],
        )

    def own_copies():
        return (
            pltpu.make_async_copy(k_ref.at[:, my_cols], k_in.at[rows_of(local, tok_rows)], k_recv.at[local]),
            pltpu.make_async_copy(v_ref.at[:, my_cols], v_in.at[rows_of(local, tok_rows)], v_recv.at[local]),
            pltpu.make_async_copy(
                q_ref.at[:, :, my_cols], q_in.at[NEAR, :, rows_of(local, rb)], q_recv.at[local]
            ),
        )

    with jax.named_scope("own"):
        for load in loads:
            load.wait()

    def to_hosts(give):
        for h, place in enumerate(places):

            @pl.when(local != place)
            def _():
                give(h, local, base + place).start()

    if split:

        @pl.when(is_upper)
        def _():
            for b in range(sent_blocks):
                for h in range(head_count):
                    give_far(h, b, local).start()

    to_hosts(give_k)
    to_hosts(give_v)
    to_hosts(give_q)

    @pl.when(is_host)
    def _():
        for copy in own_copies():
            copy.start()

    if split:

        @pl.when(is_upper)
        def _():
            for b in range(sent_blocks, blocks):
                for h in range(head_count):
                    give_far(h, b, local).start()

    wo_copy.start()

    tile_frames = min(size, 256 // rb)
    tile_rows = tile_frames * rb
    slab_frames = HEAD_DIM // rb
    slabs = tile_rows // HEAD_DIM
    span_frames = min(size, 8)
    span = span_frames * tok_rows
    key_tiles = size // span_frames
    col = lax.broadcasted_iota(jnp.int32, (1, span), 1)
    slot = col // tok_rows
    place_in = lax.rem(col, tok_rows)
    tile_row = lax.broadcasted_iota(jnp.int32, (tile_rows, 1), 0)
    ones = jnp.ones((span, HEAD_DIM), jnp.bfloat16)
    lane = lax.broadcasted_iota(jnp.int32, (tile_rows, HEAD_DIM), 1)

    def live_keys(kt):
        limit = jnp.zeros((1, span), jnp.int32)
        for f in range(span_frames):
            limit = jnp.where(slot == f, counts_ref[base + kt * span_frames + f], limit)
        return place_in < limit

    def attend(query, kind, first_frame):
        def part(kt, old_max):
            keys_at = rows_of(kt, span) if key_tiles > 1 else slice(0, span)
            scores = lax.dot_general(
                query, k_in[keys_at, :], (((1,), (1,)), ((), ())), preferred_element_type=jnp.float32
            )
            allowed = live_keys(kt)
            if kind == NEAR:
                allowed = jnp.logical_and(
                    allowed, slot + kt * span_frames <= first_frame + tile_row // rb
                )
            scores = jnp.where(allowed, scores, NEG)
            top = jnp.max(scores, axis=-1, keepdims=True)
            if old_max is not None:
                top = jnp.maximum(top, old_max)
            weights = jnp.exp2((scores - top) * scale).astype(jnp.bfloat16)
            added = jnp.dot(
                weights,
                jnp.concatenate([v_in[keys_at, :], ones], axis=1),
                preferred_element_type=jnp.float32,
            )
            return top, added

        top, acc = part(0, None)
        if key_tiles > 1:

            def more(kt, carry):
                old_max, acc = carry
                top, added = part(kt, old_max)
                return top, jnp.exp2((old_max - top) * scale) * acc + added

            top, acc = lax.fori_loop(1, key_tiles, more, (top, acc))
        return top, acc

    def answer(kind, b, j, dev):
        return (
            remote(
                acc_out.at[kind, b, rows_of(j, rb)],
                acc_in.at[kind, b, :, my_cols],
                acc_send.at[kind, b, j],
                acc_recv.at[kind, b, my_head],
                dev,
            ),
            remote(
                stat_out.at[kind, b, j // slab_frames],
                stat_in.at[kind, b, my_head],
                stat_send.at[kind, b, j],
                stat_recv.at[kind, b, my_head],
                dev,
            ),
        )

    def keep_answer(kind, b):
        return (
            pltpu.make_async_copy(
                acc_out.at[kind, b, rows_of(local, rb)],
                acc_in.at[kind, b, :, my_cols],
                acc_recv.at[kind, b, my_head],
            ),
            pltpu.make_async_copy(
                stat_out.at[kind, b, local // slab_frames],
                stat_in.at[kind, b, my_head],
                stat_recv.at[kind, b, my_head],
            ),
        )

    def serve(kind, b):
        for t in range(size // tile_frames):
            at = slice(t * tile_rows, (t + 1) * tile_rows)
            top, acc = attend(q_in[kind, b, at, :], kind, t * tile_frames)
            acc_out[kind, b, at, :] = acc[:, :HEAD_DIM].astype(jnp.bfloat16)
            stats = jnp.where(lane == 0, top, acc[:, HEAD_DIM:])
            for s in range(slabs):
                turned = jnp.transpose(stats[s * HEAD_DIM : (s + 1) * HEAD_DIM])
                stat_out[kind, b, t * slabs + s] = turned[:2]

            def send(i):
                j = t * tile_frames + i
                if kind == NEAR:

                    @pl.when(local != j)
                    def _():
                        for copy in answer(kind, b, j, base + j):
                            copy.start()

                    @pl.when(local == j)
                    def _():
                        for copy in keep_answer(kind, b):
                            copy.start()

                else:
                    for copy in answer(kind, b, j, size + j):
                        copy.start()

            each(tile_frames, send)

    @pl.when(is_host)
    def _():
        with jax.named_scope("wk"):
            each(size, lambda j: give_k(0, j, me).wait_recv())
        with jax.named_scope("wv"):
            each(size, lambda j: give_v(0, j, me).wait_recv())
        if split:

            @pl.when(jnp.logical_not(is_upper))
            def _():
                for b in range(blocks):
                    with jax.named_scope("wf"):
                        each(size, lambda j: give_far(0, b, j).wait_recv())
                    with jax.named_scope("sf"):
                        serve(FAR, b)

        with jax.named_scope("wq"):
            each(size, lambda j: give_q(0, j, me).wait_recv())
        for b in range(blocks):
            with jax.named_scope("sn"):
                serve(NEAR, b)

    row = lax.broadcasted_iota(jnp.int32, (rb, HEAD_DIM), 0)
    padding = jnp.zeros((HEAD_DIM - 2 * stat_rows.shape[2], HEAD_DIM), jnp.float32)

    def wait_answers(kind, b):
        for h in range(head_count):
            remote(
                acc_out.at[kind, b, rows_of(0, rb)],
                acc_in.at[kind, b, :, head_cols[h]],
                acc_send.at[kind, b, 0],
                acc_recv.at[kind, b, h],
                me,
            ).wait_recv()
            remote(
                stat_out.at[kind, b, 0],
                stat_in.at[kind, b, h],
                stat_send.at[kind, b, 0],
                stat_recv.at[kind, b, h],
                me,
            ).wait_recv()

    def stats_of(kind, b):
        for h in range(head_count):
            stat_rows[kind, 0, h : h + 1, :] = stat_in[kind, b, h, 0:1, :]
            stat_rows[kind, 1, h : h + 1, :] = stat_in[kind, b, h, 1:2, :]
        return stat_rows[kind, 0], stat_rows[kind, 1]

    def finish(kinds, factors, b):
        turned = jnp.transpose(jnp.concatenate(list(factors) + [padding] + ([padding[: factors[0].shape[0]]] if len(factors) == 1 else []), axis=0))
        stat_rows_t = attended_turn(turned)
        live = row + start_of(b) < counts_ref[me]
        for h in range(head_count):
            out = 0.0
            for i, kind in enumerate(kinds):
                at = i * factors[0].shape[0] + h
                out = out + stat_rows_t[:, at : at + 1] * acc_in[kind, b, :, head_cols[h]].astype(jnp.float32)
            attended[b, :, head_cols[h]] = jnp.where(live, out, 0.0).astype(jnp.bfloat16)

    def attended_turn(turned):
        at = lax.rem(local, slab_frames) * rb
        picked = turned[:rb]
        for i in range(1, slab_frames):
            picked = jnp.where(at == i * rb, turned[i * rb : (i + 1) * rb], picked)
        return picked

    def swap(b, c):
        return pltpu.make_async_remote_copy(
            src_ref=outgoing.at[b, c],
            dst_ref=incoming.at[b, c],
            send_sem=x_send_sem.at[b, c],
            recv_sem=x_recv_sem.at[b, c],
            device_id=(me, 1 - tp),
            device_id_type=MESH,
        )

    for b in range(blocks):
        with jax.named_scope("wan"):
            wait_answers(NEAR, b)

        def near_only():
            near_max, near_sum = stats_of(NEAR, b)
            finish((NEAR,), (1.0 / near_sum,), b)

        if split:

            @pl.when(is_upper)
            def _():
                with jax.named_scope("waf"):
                    wait_answers(FAR, b)
                near_max, near_sum = stats_of(NEAR, b)
                far_max, far_sum = stats_of(FAR, b)
                top = jnp.maximum(near_max, far_max)
                near = jnp.exp2((near_max - top) * scale)
                far = jnp.exp2((far_max - top) * scale)
                total = near * near_sum + far * far_sum
                finish((NEAR, FAR), (near / total, far / total), b)

            @pl.when(jnp.logical_not(is_upper))
            def _():
                near_only()

        else:
            near_only()

        if b == 0:
            wo_copy.wait()
        with jax.named_scope("proj"):
            lhs = attended[b]
            for c in range(width // chunk):
                part = jnp.dot(
                    lhs, wo_all[:, c * chunk : (c + 1) * chunk], preferred_element_type=jnp.float32
                )
                if b < sent_blocks:
                    outgoing[b, c] = part.astype(jnp.bfloat16)
                    swap(b, c).start()
                else:
                    kept[b - sent_blocks, c] = part

    with jax.named_scope("drain"):
        for h, place in enumerate(places):

            @pl.when(local != place)
            def _():
                give_k(h, local, base + place).wait_send()
                give_v(h, local, base + place).wait_send()
                give_q(h, local, base + place).wait_send()

        if split:

            @pl.when(is_upper)
            def _():
                for b in range(blocks):
                    for h in range(head_count):
                        give_far(h, b, local).wait_send()

            @pl.when(jnp.logical_and(is_host, jnp.logical_not(is_upper)))
            def _():
                for b in range(blocks):

                    def drain_far(j):
                        for copy in answer(FAR, b, j, size + j):
                            copy.wait_send()

                    each(size, drain_far)

        @pl.when(is_host)
        def _():
            for b in range(blocks):

                def drain_near(j):
                    @pl.when(local != j)
                    def _():
                        for copy in answer(NEAR, b, j, base + j):
                            copy.wait_send()

                each(size, drain_near)

    for b in range(sent_blocks):
        for c in range(width // chunk):
            with jax.named_scope("swapw"):
                swap(b, c).wait_recv()
            out_ref[b * rb : (b + 1) * rb, c * chunk : (c + 1) * chunk] = (
                kept[b, c] + incoming[b, c].astype(jnp.float32)
            ).astype(out_ref.dtype)
    with jax.named_scope("fin"):
        for b in range(sent_blocks):
            for c in range(width // chunk):
                swap(b, c).wait_send()


def on_device(queries, keys, values, wo, frame_tokens):
    tok_rows, columns = queries.shape
    width = wo.shape[1]
    n = lax.axis_size("ctx")
    half = tok_rows // 2
    chunk = 512 if width % 512 == 0 else width
    chunks = width // chunk
    head_count = columns // HEAD_DIM
    size = group_size(n)
    blocks = BLOCKS
    sent = blocks // 2
    rb = tok_rows // blocks
    slabs = size * rb // HEAD_DIM
    stat_pad = -(-head_count // 8) * 8
    vmem = pltpu.VMEM
    dma = pltpu.SemaphoreType.DMA
    return pl.pallas_call(
        functools.partial(kernel, n, chunk),
        out_shape=jax.ShapeDtypeStruct((half, width), jnp.bfloat16),
        in_specs=[
            pl.BlockSpec(memory_space=pltpu.SMEM),
            pl.BlockSpec(memory_space=pltpu.HBM),
            pl.BlockSpec(memory_space=pltpu.HBM),
            pl.BlockSpec(memory_space=pltpu.HBM),
            pl.BlockSpec(memory_space=pltpu.HBM),
        ],
        out_specs=pl.BlockSpec(memory_space=vmem),
        scratch_shapes=[
            vmem((blocks, rb, columns), jnp.bfloat16),
            vmem((tok_rows, columns), jnp.bfloat16),
            vmem((tok_rows, columns), jnp.bfloat16),
            vmem(wo.shape, jnp.bfloat16),
            vmem((size * tok_rows, HEAD_DIM), jnp.bfloat16),
            vmem((size * tok_rows, HEAD_DIM), jnp.bfloat16),
            vmem((2, blocks, size * rb, HEAD_DIM), jnp.bfloat16),
            vmem((2, blocks, size * rb, HEAD_DIM), jnp.bfloat16),
            vmem((2, blocks, slabs, 2, HEAD_DIM), jnp.float32),
            vmem((2, blocks, rb, columns), jnp.bfloat16),
            vmem((2, blocks, head_count, 2, HEAD_DIM), jnp.float32),
            vmem((2, 2, stat_pad, HEAD_DIM), jnp.float32),
            vmem((blocks, rb, columns), jnp.bfloat16),
            vmem((sent, chunks, rb, chunk), jnp.float32),
            vmem((sent, chunks, rb, chunk), jnp.bfloat16),
            vmem((sent, chunks, rb, chunk), jnp.bfloat16),
            dma((2 + blocks,)),
            dma,
            dma((head_count,)),
            dma((head_count,)),
            dma((head_count,)),
            dma((blocks, head_count)),
            dma((size,)),
            dma((size,)),
            dma((size,)),
            dma((blocks, size)),
            dma((2, blocks, size)),
            dma((2, blocks, head_count)),
            dma((2, blocks, size)),
            dma((2, blocks, head_count)),
            dma((sent, chunks)),
            dma((sent, chunks)),
        ],
        compiler_params=pltpu.CompilerParams(
            collective_id=0, has_side_effects=True, vmem_limit_bytes=52 << 20
        ),
    )(*[pltpu.with_memory_space_constraint(x, pltpu.HBM) for x in (frame_tokens, queries, keys, values, wo)])


def solution(mesh):
    in_specs = (P("ctx", "tp"), P("ctx", "tp"), P("ctx", "tp"), P("tp", None), P())
    out_specs = P(("ctx", "tp"), None)
    return jax.shard_map(
        on_device, mesh=mesh, in_specs=in_specs, out_specs=out_specs, check_vma=False
    )
```

```python
import functools
import math

import jax
import jax.numpy as jnp
from jax import lax
from jax.experimental import pallas as pl
from jax.experimental.pallas import tpu as pltpu
from jax.sharding import PartitionSpec as P

HEAD_DIM = 128
LAYER = 4
BLOCKS = 2
NEG = -1e30
MESH = pl.DeviceIdType.MESH
FAR, NEAR = 0, 1


def group_size(n):
    levels = n // LAYER
    return n // 2 if levels % 2 == 0 else n


def host_offsets(size, head_count):
    top = size // LAYER - 1
    places = []
    for h in range(head_count):
        spread = h % LAYER
        places.append((top - h // LAYER) * LAYER + (spread % 2) * (LAYER // 2) + spread // 2)
    return places


def kernel(
    n,
    chunk,
    counts_ref,
    q_hbm,
    k_hbm,
    v_hbm,
    wo_hbm,
    out_ref,
    q_ref,
    k_ref,
    v_ref,
    wo_all,
    k_in,
    v_in,
    q_in,
    acc_out,
    stat_out,
    acc_in,
    stat_in,
    stat_rows,
    attended,
    kept,
    outgoing,
    incoming,
    in_sem,
    wo_sem,
    k_send,
    v_send,
    q_send,
    far_send,
    k_recv,
    v_recv,
    q_recv,
    far_recv,
    acc_send,
    acc_recv,
    stat_send,
    stat_recv,
    x_send_sem,
    x_recv_sem,
):
    tok_rows, columns = k_hbm.shape
    head_count = columns // HEAD_DIM
    width = wo_hbm.shape[1]
    half = tok_rows // 2
    blocks = q_ref.shape[0]
    rb = q_ref.shape[1]
    sent_blocks = blocks // 2
    me = lax.axis_index("ctx")
    tp = lax.axis_index("tp")
    size = group_size(n)
    split = size < n
    upper = me // size
    base = upper * size
    local = me - base
    is_upper = upper > 0
    places = host_offsets(size, head_count)
    my_head = jnp.int32(0)
    is_host = local < 0
    for h, place in enumerate(places):
        my_head = jnp.where(local == place, h, my_head)
        is_host = jnp.logical_or(is_host, local == place)
    my_cols = pl.ds(pl.multiple_of(my_head * HEAD_DIM, HEAD_DIM), HEAD_DIM)
    head_cols = [slice(h * HEAD_DIM, (h + 1) * HEAD_DIM) for h in range(head_count)]
    scale = math.log2(math.e) / math.sqrt(HEAD_DIM)

    def start_of(b):
        side = (1 - tp) if b < sent_blocks else tp
        return pl.multiple_of(side * half + (b % sent_blocks) * rb, rb)

    def rows_of(src, rows):
        return pl.ds(pl.multiple_of(src * rows, rows), rows)

    loads = [
        pltpu.make_async_copy(k_hbm, k_ref, in_sem.at[0]),
        pltpu.make_async_copy(v_hbm, v_ref, in_sem.at[1]),
    ] + [
        pltpu.make_async_copy(q_hbm.at[pl.ds(start_of(b), rb), :], q_ref.at[b], in_sem.at[2])
        for b in range(blocks)
    ]
    for load in loads:
        load.start()

    barrier = pltpu.get_barrier_semaphore()

    def greet(dev, other_tp):
        pl.semaphore_signal(barrier, inc=1, device_id=(dev, other_tp), device_id_type=MESH)

    def each(count, body):
        if count <= 16:
            for j in range(count):
                body(j)
        else:
            lax.fori_loop(0, count, lambda j, carry: (body(j), carry)[1], 0)

    greet(me, 1 - tp)

    @pl.when(is_host)
    def _():
        def other(j):
            @pl.when(local != j)
            def _():
                greet(base + j, tp)

        each(size, other)
        if split:

            @pl.when(jnp.logical_not(is_upper))
            def _():
                each(size, lambda j: greet(size + j, tp))

    expected = 1 + head_count - is_host.astype(jnp.int32)
    if split:
        expected = expected + jnp.where(is_upper, head_count, 0)
    with jax.named_scope("bar"):
        pl.semaphore_wait(barrier, expected)

    wo_copy = pltpu.make_async_copy(wo_hbm, wo_all, wo_sem)

    def remote(src, dst, send, recv, dev):
        return pltpu.make_async_remote_copy(
            src_ref=src,
            dst_ref=dst,
            send_sem=send,
            recv_sem=recv,
            device_id=(dev, tp),
            device_id_type=MESH,
        )

    def give_k(h, frame, dev):
        return remote(
            k_ref.at[:, head_cols[h]], k_in.at[rows_of(frame, tok_rows)], k_send, k_recv, dev
        )

    def give_v(h, frame, dev):
        return remote(
            v_ref.at[:, head_cols[h]], v_in.at[rows_of(frame, tok_rows)], v_send, v_recv, dev
        )

    def give_q(h, frame, dev):
        return remote(
            q_ref.at[:, :, head_cols[h]], q_in.at[NEAR, :, rows_of(frame, rb)], q_send, q_recv, dev
        )

    def give_far(h, b, frame):
        return remote(
            q_ref.at[b, :, head_cols[h]],
            q_in.at[FAR, b, rows_of(frame, rb)],
            far_send,
            far_recv.at[b],
            places[h],
        )

    def own_copies():
        return (
            pltpu.make_async_copy(k_ref.at[:, my_cols], k_in.at[rows_of(local, tok_rows)], k_recv),
            pltpu.make_async_copy(v_ref.at[:, my_cols], v_in.at[rows_of(local, tok_rows)], v_recv),
            pltpu.make_async_copy(
                q_ref.at[:, :, my_cols], q_in.at[NEAR, :, rows_of(local, rb)], q_recv
            ),
        )

    with jax.named_scope("own"):
        for ref, i in ((k_ref, 0), (v_ref, 1), (q_ref, 2)):
            pltpu.make_async_copy(ref, ref, in_sem.at[i]).wait()

    def to_hosts(give):
        for h, place in enumerate(places):

            @pl.when(local != place)
            def _():
                give(h, local, base + place).start()

    def to_far(first, last):
        if split:

            @pl.when(is_upper)
            def _():
                for b in range(first, last):
                    for h in range(head_count):
                        give_far(h, b, local).start()

    @pl.when(is_host)
    def _():
        for copy in own_copies():
            copy.start()

    to_far(0, sent_blocks)
    to_hosts(give_k)
    to_hosts(give_q)
    to_far(sent_blocks, blocks)
    to_hosts(give_v)
    wo_copy.start()

    tile_frames = min(size, 256 // rb)
    tile_rows = tile_frames * rb
    slab_frames = HEAD_DIM // rb
    slabs = tile_rows // HEAD_DIM
    span_frames = min(size, 8)
    span = span_frames * tok_rows
    key_tiles = size // span_frames
    col = lax.broadcasted_iota(jnp.int32, (1, span), 1)
    slot = col // tok_rows
    place_in = lax.rem(col, tok_rows)
    tile_row = lax.broadcasted_iota(jnp.int32, (tile_rows, 1), 0)
    ones = jnp.ones((span, HEAD_DIM), jnp.bfloat16)
    lane = lax.broadcasted_iota(jnp.int32, (tile_rows, HEAD_DIM), 1)

    def live_keys(kt):
        limit = jnp.zeros((1, span), jnp.int32)
        for f in range(span_frames):
            limit = jnp.where(slot == f, counts_ref[base + kt * span_frames + f], limit)
        return place_in < limit

    def weigh(query, kind, first_frame, kt, old_max):
        keys_at = rows_of(kt, span) if key_tiles > 1 else slice(0, span)
        scores = lax.dot_general(
            query, k_in[keys_at, :], (((1,), (1,)), ((), ())), preferred_element_type=jnp.float32
        )
        allowed = live_keys(kt)
        if kind == NEAR:
            allowed = jnp.logical_and(allowed, slot + kt * span_frames <= first_frame + tile_row // rb)
        scores = jnp.where(allowed, scores, NEG)
        top = jnp.max(scores, axis=-1, keepdims=True)
        if old_max is not None:
            top = jnp.maximum(top, old_max)
        return top, jnp.exp2((scores - top) * scale).astype(jnp.bfloat16)

    def gather(weights, kt):
        keys_at = rows_of(kt, span) if key_tiles > 1 else slice(0, span)
        return jnp.dot(
            weights,
            jnp.concatenate([v_in[keys_at, :], ones], axis=1),
            preferred_element_type=jnp.float32,
        )

    def more_keys(query, kind, first_frame, top, acc):
        if key_tiles == 1:
            return top, acc

        def more(kt, carry):
            old_max, acc = carry
            top, weights = weigh(query, kind, first_frame, kt, old_max)
            return top, jnp.exp2((old_max - top) * scale) * acc + gather(weights, kt)

        return lax.fori_loop(1, key_tiles, more, (top, acc))

    def answer(kind, b, j, dev):
        return (
            remote(
                acc_out.at[kind, b, rows_of(j, rb)],
                acc_in.at[kind, b, :, my_cols],
                acc_send.at[kind],
                acc_recv.at[kind, b],
                dev,
            ),
            remote(
                stat_out.at[kind, b, j // slab_frames],
                stat_in.at[kind, b, my_head],
                stat_send.at[kind],
                stat_recv.at[kind, b],
                dev,
            ),
        )

    def keep_answer(kind, b):
        return (
            pltpu.make_async_copy(
                acc_out.at[kind, b, rows_of(local, rb)],
                acc_in.at[kind, b, :, my_cols],
                acc_recv.at[kind, b],
            ),
            pltpu.make_async_copy(
                stat_out.at[kind, b, local // slab_frames],
                stat_in.at[kind, b, my_head],
                stat_recv.at[kind, b],
            ),
        )

    tiles = size // tile_frames

    def query_at(kind, b, t):
        return q_in[kind, b, t * tile_rows : (t + 1) * tile_rows, :]

    def begin(kind, b, t):
        return weigh(query_at(kind, b, t), kind, t * tile_frames, 0, None)

    def serve(kind, b, t, begun):
        top, weights = begun
        top, acc = more_keys(query_at(kind, b, t), kind, t * tile_frames, top, gather(weights, 0))
        acc_out[kind, b, t * tile_rows : (t + 1) * tile_rows, :] = acc[:, :HEAD_DIM].astype(jnp.bfloat16)
        stats = jnp.where(lane == 0, top, acc[:, HEAD_DIM:])
        for s in range(slabs):
            turned = jnp.transpose(stats[s * HEAD_DIM : (s + 1) * HEAD_DIM])
            stat_out[kind, b, t * slabs + s] = turned[:2]

        def send(i):
            j = (t + 1) * tile_frames - 1 - i
            if kind == NEAR:

                @pl.when(local != j)
                def _():
                    for copy in answer(kind, b, j, base + j):
                        copy.start()

                @pl.when(local == j)
                def _():
                    for copy in keep_answer(kind, b):
                        copy.start()

            else:
                for copy in answer(kind, b, j, size + j):
                    copy.start()

        each(tile_frames, send)

    def arrived(ref, sem):
        pltpu.make_async_copy(ref, ref, sem).wait()

    @pl.when(is_host)
    def _():
        with jax.named_scope("wk"):
            arrived(k_in, k_recv)
        with jax.named_scope("wq"):
            arrived(q_in.at[NEAR], q_recv)
        first = tiles == 1 and key_tiles == 1
        with jax.named_scope("beg"):
            begun = [begin(NEAR, b, 0) for b in range(blocks)] if first else None
        with jax.named_scope("wv"):
            arrived(v_in, v_recv)
        with jax.named_scope("sn"):
            for b in range(blocks):
                for t in range(tiles):
                    serve(NEAR, b, t, begun[b] if first else begin(NEAR, b, t))
        if split:

            @pl.when(jnp.logical_not(is_upper))
            def _():
                for b in range(blocks):
                    with jax.named_scope("wf"):
                        arrived(q_in.at[FAR, b], far_recv.at[b])
                    with jax.named_scope("sf"):
                        for t in range(tiles):
                            serve(FAR, b, t, begin(FAR, b, t))

    row = lax.broadcasted_iota(jnp.int32, (rb, HEAD_DIM), 0)
    padding = jnp.zeros((HEAD_DIM - 2 * stat_rows.shape[2], HEAD_DIM), jnp.float32)

    def wait_answers(kind, b):
        arrived(acc_in.at[kind, b], acc_recv.at[kind, b])
        arrived(stat_in.at[kind, b], stat_recv.at[kind, b])

    def stats_of(kind, b):
        for h in range(head_count):
            stat_rows[kind, 0, h : h + 1, :] = stat_in[kind, b, h, 0:1, :]
            stat_rows[kind, 1, h : h + 1, :] = stat_in[kind, b, h, 1:2, :]
        return stat_rows[kind, 0], stat_rows[kind, 1]

    def finish(kinds, factors, b):
        turned = jnp.transpose(jnp.concatenate(list(factors) + [padding] + ([padding[: factors[0].shape[0]]] if len(factors) == 1 else []), axis=0))
        stat_rows_t = attended_turn(turned)
        live = row + start_of(b) < counts_ref[me]
        for h in range(head_count):
            out = 0.0
            for i, kind in enumerate(kinds):
                at = i * factors[0].shape[0] + h
                out = out + stat_rows_t[:, at : at + 1] * acc_in[kind, b, :, head_cols[h]].astype(jnp.float32)
            attended[b, :, head_cols[h]] = jnp.where(live, out, 0.0).astype(jnp.bfloat16)

    def attended_turn(turned):
        at = lax.rem(local, slab_frames) * rb
        picked = turned[:rb]
        for i in range(1, slab_frames):
            picked = jnp.where(at == i * rb, turned[i * rb : (i + 1) * rb], picked)
        return picked

    def swap(b, c):
        return pltpu.make_async_remote_copy(
            src_ref=outgoing.at[b, c],
            dst_ref=incoming.at[b, c],
            send_sem=x_send_sem,
            recv_sem=x_recv_sem.at[b, c],
            device_id=(me, 1 - tp),
            device_id_type=MESH,
        )

    for b in range(blocks):
        with jax.named_scope("wan"):
            wait_answers(NEAR, b)

        def near_only():
            near_max, near_sum = stats_of(NEAR, b)
            finish((NEAR,), (1.0 / near_sum,), b)

        if split:

            @pl.when(is_upper)
            def _():
                with jax.named_scope("waf"):
                    wait_answers(FAR, b)
                near_max, near_sum = stats_of(NEAR, b)
                far_max, far_sum = stats_of(FAR, b)
                top = jnp.maximum(near_max, far_max)
                near = jnp.exp2((near_max - top) * scale)
                far = jnp.exp2((far_max - top) * scale)
                total = near * near_sum + far * far_sum
                finish((NEAR, FAR), (near / total, far / total), b)

            @pl.when(jnp.logical_not(is_upper))
            def _():
                near_only()

        else:
            near_only()

        if b == 0:
            wo_copy.wait()
        with jax.named_scope("proj"):
            lhs = attended[b]
            for c in range(width // chunk):
                part = jnp.dot(
                    lhs, wo_all[:, c * chunk : (c + 1) * chunk], preferred_element_type=jnp.float32
                )
                if b < sent_blocks:
                    outgoing[b, c] = part.astype(jnp.bfloat16)
                    swap(b, c).start()
                else:
                    kept[b - sent_blocks, c] = part

    def left(ref, sem):
        pltpu.make_async_copy(ref, ref, sem).wait()

    def answers_left(kind, count):
        left(acc_out.at[kind, :, : count * rb], acc_send.at[kind])
        bits = stat_out.shape[3] * 2
        left(acc_out.at[kind, :, : count * bits], stat_send.at[kind])

    with jax.named_scope("drain"):

        def gifts_left(count):
            left(k_ref.at[:, : count * HEAD_DIM], k_send)
            left(v_ref.at[:, : count * HEAD_DIM], v_send)
            left(q_ref.at[:, :, : count * HEAD_DIM], q_send)

        @pl.when(is_host)
        def _():
            gifts_left(head_count - 1)
            answers_left(NEAR, size - 1)

        @pl.when(jnp.logical_not(is_host))
        def _():
            gifts_left(head_count)

        if split:

            @pl.when(is_upper)
            def _():
                left(q_ref, far_send)

            @pl.when(jnp.logical_and(is_host, jnp.logical_not(is_upper)))
            def _():
                answers_left(FAR, size)

    for b in range(sent_blocks):
        for c in range(width // chunk):
            with jax.named_scope("swapw"):
                swap(b, c).wait_recv()
            out_ref[b * rb : (b + 1) * rb, c * chunk : (c + 1) * chunk] = (
                kept[b, c] + incoming[b, c].astype(jnp.float32)
            ).astype(out_ref.dtype)
    with jax.named_scope("fin"):
        left(outgoing, x_send_sem)


def on_device(queries, keys, values, wo, frame_tokens):
    tok_rows, columns = queries.shape
    width = wo.shape[1]
    n = lax.axis_size("ctx")
    half = tok_rows // 2
    chunk = 512 if width % 512 == 0 else width
    chunks = width // chunk
    head_count = columns // HEAD_DIM
    size = group_size(n)
    blocks = BLOCKS
    sent = blocks // 2
    rb = tok_rows // blocks
    slabs = size * rb // HEAD_DIM
    stat_pad = -(-head_count // 8) * 8
    vmem = pltpu.VMEM
    dma = pltpu.SemaphoreType.DMA
    return pl.pallas_call(
        functools.partial(kernel, n, chunk),
        out_shape=jax.ShapeDtypeStruct((half, width), jnp.bfloat16),
        in_specs=[
            pl.BlockSpec(memory_space=pltpu.SMEM),
            pl.BlockSpec(memory_space=pltpu.HBM),
            pl.BlockSpec(memory_space=pltpu.HBM),
            pl.BlockSpec(memory_space=pltpu.HBM),
            pl.BlockSpec(memory_space=pltpu.HBM),
        ],
        out_specs=pl.BlockSpec(memory_space=vmem),
        scratch_shapes=[
            vmem((blocks, rb, columns), jnp.bfloat16),
            vmem((tok_rows, columns), jnp.bfloat16),
            vmem((tok_rows, columns), jnp.bfloat16),
            vmem(wo.shape, jnp.bfloat16),
            vmem((size * tok_rows, HEAD_DIM), jnp.bfloat16),
            vmem((size * tok_rows, HEAD_DIM), jnp.bfloat16),
            vmem((2, blocks, size * rb, HEAD_DIM), jnp.bfloat16),
            vmem((2, blocks, size * rb, HEAD_DIM), jnp.bfloat16),
            vmem((2, blocks, slabs, 2, HEAD_DIM), jnp.float32),
            vmem((2, blocks, rb, columns), jnp.bfloat16),
            vmem((2, blocks, head_count, 2, HEAD_DIM), jnp.float32),
            vmem((2, 2, stat_pad, HEAD_DIM), jnp.float32),
            vmem((blocks, rb, columns), jnp.bfloat16),
            vmem((sent, chunks, rb, chunk), jnp.float32),
            vmem((sent, chunks, rb, chunk), jnp.bfloat16),
            vmem((sent, chunks, rb, chunk), jnp.bfloat16),
            dma((3,)),
            dma,
            dma,
            dma,
            dma,
            dma,
            dma,
            dma,
            dma,
            dma((blocks,)),
            dma((2,)),
            dma((2, blocks)),
            dma((2,)),
            dma((2, blocks)),
            dma,
            dma((sent, chunks)),
        ],
        compiler_params=pltpu.CompilerParams(
            collective_id=0, has_side_effects=True, vmem_limit_bytes=52 << 20
        ),
    )(*[pltpu.with_memory_space_constraint(x, pltpu.HBM) for x in (frame_tokens, queries, keys, values, wo)])


def solution(mesh):
    in_specs = (P("ctx", "tp"), P("ctx", "tp"), P("ctx", "tp"), P("tp", None), P())
    out_specs = P(("ctx", "tp"), None)
    return jax.shard_map(
        on_device, mesh=mesh, in_specs=in_specs, out_specs=out_specs, check_vma=False
    )
```

```python
import functools
import math

import jax
import jax.numpy as jnp
from jax import lax
from jax.experimental import pallas as pl
from jax.experimental.pallas import tpu as pltpu
from jax.sharding import PartitionSpec as P

HEAD_DIM = 128
LAYER = 4
NEG = -1e30
MESH = pl.DeviceIdType.MESH
FAR, NEAR = 0, 1
STAT_ROWS = 8


def group_size(n):
    levels = n // LAYER
    return n // 2 if levels % 2 == 0 else n


def host_places(size, head_count):
    top = size - LAYER
    order = [top + i for i in (0, 2, 1, 3)] + list(range(top))
    return order[:head_count]


def kernel(
    n,
    chunk,
    counts_ref,
    q_hbm,
    k_hbm,
    v_hbm,
    wo_hbm,
    out_ref,
    q_ref,
    k_pal,
    v_pal,
    wo_all,
    k_in,
    v_in,
    q_in,
    acc_out,
    stat_out,
    acc_in,
    stat_in,
    stat_rows,
    near_stat,
    attended,
    kept,
    outgoing,
    incoming,
    in_sem,
    wo_sem,
    k_send,
    v_send,
    q_send,
    far_send,
    k_recv,
    v_recv,
    q_recv,
    far_recv,
    pal_send,
    pal_recv,
    acc_send,
    acc_recv,
    stat_send,
    stat_recv,
    x_send_sem,
    x_recv_sem,
):
    tok_rows, columns = k_hbm.shape
    head_count = columns // HEAD_DIM
    width = wo_hbm.shape[1]
    half = tok_rows // 2
    quarter = half // 2
    chunks = width // chunk
    parts = [(0, quarter), (quarter, quarter), (half, half)]
    me = lax.axis_index("ctx")
    tp = lax.axis_index("tp")
    size = group_size(n)
    split = size < n
    upper = me // size
    base = upper * size
    local = me - base
    is_upper = upper > 0
    is_lower = jnp.logical_not(is_upper)
    is_base = local < LAYER
    is_top = jnp.logical_not(is_base)
    lane = lax.rem(me, LAYER)
    places = host_places(size, head_count)
    my_head = jnp.int32(0)
    is_host = local < 0
    for h, place in enumerate(places):
        my_head = jnp.where(local == place, h, my_head)
        is_host = jnp.logical_or(is_host, local == place)
    my_cols = pl.ds(pl.multiple_of(my_head * HEAD_DIM, HEAD_DIM), HEAD_DIM)
    head_cols = [slice(h * HEAD_DIM, (h + 1) * HEAD_DIM) for h in range(head_count)]
    scale = math.log2(math.e) / math.sqrt(HEAD_DIM)

    def both(a, b):
        return jnp.logical_and(a, b)

    def start_of(b):
        return pl.multiple_of((1 - tp if b == 0 else tp) * half, half)

    def rows_of(src, rows):
        return pl.ds(pl.multiple_of(src * rows, rows), rows)

    pltpu.make_async_copy(k_hbm, k_pal.at[lane], in_sem.at[0]).start()
    pltpu.make_async_copy(v_hbm, v_pal.at[lane], in_sem.at[1]).start()
    for b in range(2):
        pltpu.make_async_copy(q_hbm.at[pl.ds(start_of(b), half), :], q_ref.at[b], in_sem.at[2]).start()

    wo_copy = pltpu.make_async_copy(wo_hbm, wo_all, wo_sem)
    first_pair = both(both(is_base, is_lower), lane < 2)
    pl.when(first_pair)(wo_copy.start)
    barrier = pltpu.get_barrier_semaphore()

    def greet(dev, other_tp):
        pl.semaphore_signal(barrier, inc=1, device_id=(dev, other_tp), device_id_type=MESH)

    def each(count, body):
        if count <= 16:
            for j in range(count):
                body(j)
        else:
            lax.fori_loop(0, count, lambda j, carry: (body(j), carry)[1], 0)

    greet(me, 1 - tp)
    takes = {1: (0,), 2: (0, 3), 3: (1, 2)}
    for to, sources in takes.items():

        @pl.when(both(is_base, lane == to))
        def _():
            for source in sources:
                greet(base + source, tp)

    @pl.when(is_host)
    def _():
        def other(j):
            @pl.when(local != j)
            def _():
                greet(base + j, tp)

        each(size, other)
        if split:

            @pl.when(is_lower)
            def _():
                each(size, lambda j: greet(size + j, tp))

    gifts = jnp.where(lane == 0, 2, 1)
    expected = 1 + head_count - is_host.astype(jnp.int32) + jnp.where(is_base, gifts, 0)
    if split:
        expected = expected + jnp.where(is_upper, head_count, 0)
    with jax.named_scope("bar"):
        pl.semaphore_wait(barrier, expected)

    def remote(src, dst, send, recv, dev):
        return pltpu.make_async_remote_copy(
            src_ref=src,
            dst_ref=dst,
            send_sem=send,
            recv_sem=recv,
            device_id=(dev, tp),
            device_id_type=MESH,
        )

    def arrived(ref, sem):
        pltpu.make_async_copy(ref, ref, sem).wait()

    def give_k(h, dev):
        return remote(k_pal.at[lane, :, head_cols[h]], k_in.at[rows_of(local, tok_rows)], k_send, k_recv, dev)

    def give_v(h, dev):
        return remote(v_pal.at[lane, :, head_cols[h]], v_in.at[rows_of(local, tok_rows)], v_send, v_recv, dev)

    def give_q(h, dev):
        return remote(q_ref.at[:, :, head_cols[h]], q_in.at[NEAR, :, rows_of(local, half)], q_send, q_recv, dev)

    def give_far(h, b):
        return remote(
            q_ref.at[b, :, head_cols[h]],
            q_in.at[FAR, b, rows_of(local, half)],
            far_send,
            far_recv.at[b],
            places[h],
        )

    def pal(kind, frame, to):
        ref = (k_pal, v_pal)[kind].at[frame]
        return remote(ref, ref, pal_send, pal_recv.at[kind, frame], base + to)

    with jax.named_scope("own"):
        arrived(k_pal.at[lane], in_sem.at[0])
        arrived(v_pal.at[lane], in_sem.at[1])
        arrived(q_ref, in_sem.at[2])

    def to_hosts(give):
        for h in nearest_last:
            place = places[h]

            @pl.when(local != place)
            def _():
                give(h, base + place).start()

    nearest_last = sorted(range(head_count), key=lambda h: places[h])

    def to_far(b, who):
        if split:

            @pl.when(both(is_upper, who))
            def _():
                for h in nearest_last:
                    give_far(h, b).start()

    @pl.when(both(is_base, lane == 0))
    def _():
        for kind in range(2):
            pal(kind, 0, 1).start()

    @pl.when(both(is_base, lane == 2))
    def _():
        for kind in range(2):
            pal(kind, 2, 3).start()

    to_far(0, is_upper)
    to_far(1, is_base)
    to_hosts(give_k)

    @pl.when(both(is_upper, is_top))
    def _():
        to_hosts(give_q)

    to_hosts(give_v)
    to_far(1, is_top)

    @pl.when(is_host)
    def _():
        pltpu.make_async_copy(k_pal.at[lane, :, my_cols], k_in.at[rows_of(local, tok_rows)], k_recv).start()
        pltpu.make_async_copy(v_pal.at[lane, :, my_cols], v_in.at[rows_of(local, tok_rows)], v_recv).start()

        @pl.when(is_top)
        def _():
            pltpu.make_async_copy(
                q_ref.at[:, :, my_cols], q_in.at[NEAR, :, rows_of(local, half)], q_recv
            ).start()

    @pl.when(both(is_lower, is_top))
    def _():
        to_hosts(give_q)

    for kind in range(2):
        for source in range(2):

            @pl.when(both(is_base, lane == source))
            def _():
                pal(kind, source, source + 2).start()

    pl.when(jnp.logical_not(first_pair))(wo_copy.start)

    def masked_weights(scores, allowed):
        scores = jnp.where(allowed, scores, NEG)
        top = jnp.max(scores, axis=-1, keepdims=True)
        return top, jnp.exp2((scores - top) * scale).astype(jnp.bfloat16)

    def attend_level():
        col = lax.broadcasted_iota(jnp.int32, (1, LAYER * tok_rows), 1)
        slot = col // tok_rows
        limit = jnp.zeros(col.shape, jnp.int32)
        for f in range(LAYER):
            limit = jnp.where(slot == f, jnp.where(f <= lane, counts_ref[base + f], 0), limit)
        allowed = lax.rem(col, tok_rows) < limit
        ones = jnp.ones((LAYER * tok_rows, HEAD_DIM), jnp.bfloat16)
        frames = [jnp.minimum(f, lane) for f in range(LAYER)]
        at = lax.broadcasted_iota(jnp.int32, (tok_rows, HEAD_DIM), 1)
        begun = []
        for cols in head_cols:
            query = jnp.concatenate([q_ref[0, :, cols], q_ref[1, :, cols]], axis=0)
            keys = jnp.concatenate([k_pal[f, :, cols] for f in frames], axis=0)
            scores = lax.dot_general(
                query, keys, (((1,), (1,)), ((), ())), preferred_element_type=jnp.float32
            )
            begun.append(masked_weights(scores, allowed))
        stats = jnp.zeros((tok_rows, HEAD_DIM), jnp.float32)
        for h, cols in enumerate(head_cols):
            top, weights = begun[h]
            vals = jnp.concatenate([v_pal[f, :, cols] for f in frames], axis=0)
            acc = jnp.dot(weights, jnp.concatenate([vals, ones], axis=1), preferred_element_type=jnp.float32)
            acc_in[NEAR, :, cols] = acc[:, :HEAD_DIM].astype(jnp.bfloat16)
            stats = jnp.where(at == h, top, stats)
            stats = jnp.where(at == STAT_ROWS + h, acc[:, HEAD_DIM:], stats)
        near_stat[:tok_rows, :] = stats

    far_frames = min(size, 256 // half)
    near_frames = min(size - LAYER, HEAD_DIM // half)
    slab_frames = HEAD_DIM // half
    span_frames = min(size, 8)
    span = span_frames * tok_rows
    key_tiles = size // span_frames
    col = lax.broadcasted_iota(jnp.int32, (1, span), 1)
    slot = col // tok_rows
    place_in = lax.rem(col, tok_rows)
    ones = jnp.ones((span, HEAD_DIM), jnp.bfloat16)

    def keys_at(kt):
        return rows_of(kt, span) if key_tiles > 1 else slice(0, span)

    def weigh(query, row_frame, kt, old_max):
        scores = lax.dot_general(
            query, k_in[keys_at(kt), :], (((1,), (1,)), ((), ())), preferred_element_type=jnp.float32
        )
        limit = jnp.zeros((1, span), jnp.int32)
        for f in range(span_frames):
            limit = jnp.where(slot == f, counts_ref[base + kt * span_frames + f], limit)
        allowed = place_in < limit
        if row_frame is not None:
            allowed = jnp.logical_and(allowed, slot + kt * span_frames <= row_frame)
        scores = jnp.where(allowed, scores, NEG)
        top = jnp.max(scores, axis=-1, keepdims=True)
        if old_max is not None:
            top = jnp.maximum(top, old_max)
        return top, jnp.exp2((scores - top) * scale).astype(jnp.bfloat16)

    def gather(weights, kt):
        return jnp.dot(
            weights,
            jnp.concatenate([v_in[keys_at(kt), :], ones], axis=1),
            preferred_element_type=jnp.float32,
        )

    def more_keys(query, row_frame, top, acc):
        if key_tiles == 1:
            return top, acc

        def more(kt, carry):
            old_max, acc = carry
            top, weights = weigh(query, row_frame, kt, old_max)
            return top, jnp.exp2((old_max - top) * scale) * acc + gather(weights, kt)

        return lax.fori_loop(1, key_tiles, more, (top, acc))

    def begin(query, row_frame):
        return query, row_frame, weigh(query, row_frame, 0, None)

    def end(begun):
        query, row_frame, (top, weights) = begun
        return more_keys(query, row_frame, top, gather(weights, 0))

    def acc_copies(kind, p, j, dev):
        first, rows = parts[p]
        b = first // half
        src = acc_out.at[kind, b, pl.ds(j * half + first - b * half, rows)]
        dst = acc_in.at[kind, pl.ds(first, rows), my_cols]
        return src, dst, acc_send.at[kind], acc_recv.at[kind, p], dev

    def stat_copies(kind, b, j, dev):
        return (
            stat_out.at[kind, b, j // slab_frames],
            stat_in.at[kind, b, my_head],
            stat_send.at[kind],
            stat_recv.at[kind, b],
            dev,
        )

    def post(kind, copy, frames):
        for j in frames:
            if kind == FAR:
                remote(*copy(j, size + j)).start()
            else:
                src, dst, send, recv, dev = copy(j, base + j)

                @pl.when(local != j)
                def _():
                    remote(src, dst, send, recv, dev).start()

                @pl.when(local == j)
                def _():
                    pltpu.make_async_copy(src, dst, recv).start()

    def stats_from(kind, b, first, top, acc):
        at = lax.broadcasted_iota(jnp.int32, acc[:, HEAD_DIM:].shape, 1)
        stats = jnp.where(at == 0, top, acc[:, HEAD_DIM:])
        for s in range(stats.shape[0] // HEAD_DIM):
            turned = jnp.transpose(stats[s * HEAD_DIM : (s + 1) * HEAD_DIM])
            stat_out[kind, b, first // slab_frames + s] = turned[:2]

    def begin_far(b, t):
        return begin(q_in[FAR, b, t * far_frames * half : (t + 1) * far_frames * half, :], None)

    def serve_far(b, t, begun):
        top, acc = end(begun)
        first = t * far_frames
        acc_out[FAR, b, first * half : (first + far_frames) * half, :] = acc[:, :HEAD_DIM].astype(jnp.bfloat16)
        frames = range(first + far_frames - 1, first - 1, -1)
        mine = [p for p, (at, rows) in enumerate(parts) if at // half == b]
        post(FAR, lambda j, dev: acc_copies(FAR, mine[0], j, dev), frames)
        stats_from(FAR, b, first, top, acc)
        post(FAR, lambda j, dev: stat_copies(FAR, b, j, dev), frames)
        for p in mine[1:]:
            post(FAR, lambda j, dev: acc_copies(FAR, p, j, dev), frames)

    near_rows = near_frames * half
    near_tiles = (size - LAYER) // near_frames

    def near_at(t):
        first = LAYER + t * near_frames
        return first, slice(first * half, (first + near_frames) * half)

    def begin_near(t):
        first, at = near_at(t)
        row = lax.broadcasted_iota(jnp.int32, (2 * near_rows, 1), 0)
        query = jnp.concatenate([q_in[NEAR, 0, at, :], q_in[NEAR, 1, at, :]], axis=0)
        return begin(query, first + lax.rem(row, near_rows) // half)

    def serve_near(t, begun):
        top, acc = end(begun)
        first, at = near_at(t)
        for b in range(2):
            rows = slice(b * near_rows, (b + 1) * near_rows)
            acc_out[NEAR, b, at, :] = acc[rows, :HEAD_DIM].astype(jnp.bfloat16)
        frames = range(first + near_frames - 1, first - 1, -1)
        post(NEAR, lambda j, dev: acc_copies(NEAR, 0, j, dev), frames)
        for b in range(2):
            rows = slice(b * near_rows, (b + 1) * near_rows)
            stats_from(NEAR, b, first, top[rows], acc[rows])
            post(NEAR, lambda j, dev: stat_copies(NEAR, b, j, dev), frames)
        for p in (1, 2):
            post(NEAR, lambda j, dev: acc_copies(NEAR, p, j, dev), frames)

    def serve_all_near(begun):
        with jax.named_scope("sn"):
            for t in range(near_tiles):
                serve_near(t, begun if begun is not None else begin_near(t))

    def serve_all_far(b, begun):
        with jax.named_scope("sf"):
            for t in range(size // far_frames):
                serve_far(b, t, begun if begun is not None else begin_far(b, t))

    def host():
        with jax.named_scope("wk"):
            arrived(k_in, k_recv)

        def wait_near():
            with jax.named_scope("wq"):
                arrived(q_in.at[NEAR, :, LAYER * half :], q_recv)

        def host_near():
            wait_near()
            with jax.named_scope("bn"):
                begun = begin_near(0) if near_tiles == 1 and key_tiles == 1 else None
            with jax.named_scope("wv"):
                arrived(v_in, v_recv)
            serve_all_near(begun)

        def host_both():
            with jax.named_scope("wf"):
                arrived(q_in.at[FAR, 0], far_recv.at[0])
            with jax.named_scope("bf"):
                begun = begin_far(0, 0) if size == far_frames and key_tiles == 1 else None
            with jax.named_scope("wv"):
                arrived(v_in, v_recv)
            serve_all_far(0, begun)
            wait_near()
            serve_all_near(None)
            with jax.named_scope("wf"):
                arrived(q_in.at[FAR, 1], far_recv.at[1])
            serve_all_far(1, None)

        if split:
            pl.when(is_lower)(host_both)
            pl.when(is_upper)(host_near)
        else:
            host_near()

    lead = lax.rem(local, slab_frames) * half
    row = lax.broadcasted_iota(jnp.int32, (half, HEAD_DIM), 0)
    padding = jnp.zeros((HEAD_DIM - 2 * STAT_ROWS, HEAD_DIM), jnp.float32)

    def stat_columns(kind, b):
        for h in range(head_count):
            stat_rows[kind, h : h + 1, :] = stat_in[kind, b, h, 0:1, :]
            stat_rows[kind, STAT_ROWS + h : STAT_ROWS + h + 1, :] = stat_in[kind, b, h, 1:2, :]
        turned = jnp.transpose(jnp.concatenate([stat_rows[kind], padding], axis=0))
        picked = turned[:half]
        for i in range(1, slab_frames):
            picked = jnp.where(lead == i * half, turned[i * half : (i + 1) * half], picked)
        return picked

    def sums(stats):
        return pltpu.roll(stats, HEAD_DIM - STAT_ROWS, 1)

    def swap(p, c):
        first, rows = parts[p]
        return pltpu.make_async_remote_copy(
            src_ref=outgoing.at[p, c],
            dst_ref=incoming.at[p, c],
            send_sem=x_send_sem,
            recv_sem=x_recv_sem.at[p, c],
            device_id=(me, 1 - tp),
            device_id_type=MESH,
        )

    def own_rows(which, from_hosts, from_far):
        for p in which:
            first, rows = parts[p]
            b = first // half
            if from_hosts:

                @pl.when(is_top)
                def _():
                    with jax.named_scope("wan"):
                        arrived(acc_in.at[NEAR, pl.ds(first, rows)], acc_recv.at[NEAR, p])
                        if first % half == 0:
                            arrived(stat_in.at[NEAR, b], stat_recv.at[NEAR, b])
                            near_stat[b * half : (b + 1) * half, :] = stat_columns(NEAR, b)

            live = row[:rows] + (start_of(b) + first - b * half) < counts_ref[me]

            def merge(far):
                near = near_stat[first : first + rows, :]
                if far:
                    other = near_stat[tok_rows + first : tok_rows + first + rows, :]
                    top = jnp.maximum(near, other)
                    near_part = jnp.exp2((near - top) * scale)
                    far_part = jnp.exp2((other - top) * scale)
                    total = near_part * sums(near) + far_part * sums(other)
                    factors = ((NEAR, near_part / total), (FAR, far_part / total))
                else:
                    factors = ((NEAR, 1.0 / sums(near)),)
                for h, cols in enumerate(head_cols):
                    out = 0.0
                    for kind, factor in factors:
                        out = out + factor[:, h : h + 1] * acc_in[kind, first : first + rows, cols].astype(
                            jnp.float32
                        )
                    attended[first : first + rows, cols] = jnp.where(live, out, 0.0).astype(jnp.bfloat16)

            if from_far:

                @pl.when(is_upper)
                def _():
                    with jax.named_scope("waf"):
                        arrived(acc_in.at[FAR, pl.ds(first, rows)], acc_recv.at[FAR, p])
                        if first % half == 0:
                            arrived(stat_in.at[FAR, b], stat_recv.at[FAR, b])
                            near_stat[tok_rows + b * half : tok_rows + (b + 1) * half, :] = stat_columns(FAR, b)
                    merge(True)

                @pl.when(is_lower)
                def _():
                    merge(False)

            else:
                merge(False)

            if p == 0:
                wo_copy.wait()
            with jax.named_scope("proj"):
                lhs = attended[first : first + rows, :]
                for c in range(chunks):
                    part = jnp.dot(
                        lhs, wo_all[:, c * chunk : (c + 1) * chunk], preferred_element_type=jnp.float32
                    )
                    if b == 0:
                        outgoing[p, c] = part.astype(jnp.bfloat16)
                        swap(p, c).start()
                    else:
                        kept[:, c * chunk : (c + 1) * chunk] = part

    @pl.when(is_base)
    def _():
        def pass_on(frame, to):
            for kind in range(2):
                arrived((k_pal, v_pal)[kind].at[frame], pal_recv.at[kind, frame])
                if to is not None:
                    pal(kind, frame, to).start()

        with jax.named_scope("pal"):

            @pl.when(lane == 1)
            def _():
                pass_on(0, None)

            @pl.when(lane == 2)
            def _():
                pass_on(0, 3)
                pass_on(1, None)

            @pl.when(lane == 3)
            def _():
                pass_on(1, 2)
                pass_on(2, None)
                pass_on(0, None)

        with jax.named_scope("lev"):
            attend_level()

        @pl.when(is_lower)
        def _():
            own_rows((0,), False, False)

    pl.when(is_host)(host)

    @pl.when(both(is_base, is_lower))
    def _():
        own_rows((1, 2), False, False)

    @pl.when(jnp.logical_not(both(is_base, is_lower)))
    def _():
        own_rows((0, 1, 2), True, split)

    with jax.named_scope("drain"):

        def given(count):
            arrived(k_pal.at[0, :, : count * HEAD_DIM], k_send)
            arrived(v_pal.at[0, :, : count * HEAD_DIM], v_send)

            @pl.when(is_top)
            def _():
                arrived(q_ref.at[:, :, : count * HEAD_DIM], q_send)

        def answered(kind, count):
            arrived(acc_out.at[kind, :, : count * half], acc_send.at[kind])
            arrived(acc_out.at[kind, :, : count * 4], stat_send.at[kind])

        @pl.when(is_host)
        def _():
            given(head_count - 1)

            @pl.when(is_top)
            def _():
                answered(NEAR, size - LAYER - 1)

            @pl.when(is_base)
            def _():
                answered(NEAR, size - LAYER)

            if split:

                @pl.when(is_lower)
                def _():
                    answered(FAR, size)

        @pl.when(jnp.logical_not(is_host))
        def _():
            given(head_count)

        if split:

            @pl.when(is_upper)
            def _():
                arrived(q_ref, far_send)

        for lanes, count in (((0, 2), 2), ((1, 3), 1)):

            @pl.when(both(is_base, jnp.logical_or(lane == lanes[0], lane == lanes[1])))
            def _():
                arrived(k_pal.at[: 2 * count], pal_send)

    for c in range(chunks):
        at = slice(c * chunk, (c + 1) * chunk)
        for p in range(2):
            first, rows = parts[p]
            with jax.named_scope("swapw"):
                arrived(incoming.at[p, c], x_recv_sem.at[p, c])
            out_ref[first : first + rows, at] = (
                kept[first : first + rows, at] + incoming[p, c].astype(jnp.float32)
            ).astype(out_ref.dtype)
    with jax.named_scope("fin"):
        arrived(outgoing, x_send_sem)


def on_device(queries, keys, values, wo, frame_tokens):
    tok_rows, columns = queries.shape
    width = wo.shape[1]
    n = lax.axis_size("ctx")
    half = tok_rows // 2
    chunk = 512 if width % 512 == 0 else width
    chunks = width // chunk
    head_count = columns // HEAD_DIM
    size = group_size(n)
    slabs = size * half // HEAD_DIM
    vmem = pltpu.VMEM
    dma = pltpu.SemaphoreType.DMA
    return pl.pallas_call(
        functools.partial(kernel, n, chunk),
        out_shape=jax.ShapeDtypeStruct((half, width), jnp.bfloat16),
        in_specs=[
            pl.BlockSpec(memory_space=pltpu.SMEM),
            pl.BlockSpec(memory_space=pltpu.HBM),
            pl.BlockSpec(memory_space=pltpu.HBM),
            pl.BlockSpec(memory_space=pltpu.HBM),
            pl.BlockSpec(memory_space=pltpu.HBM),
        ],
        out_specs=pl.BlockSpec(memory_space=vmem),
        scratch_shapes=[
            vmem((2, half, columns), jnp.bfloat16),
            vmem((LAYER, tok_rows, columns), jnp.bfloat16),
            vmem((LAYER, tok_rows, columns), jnp.bfloat16),
            vmem(wo.shape, jnp.bfloat16),
            vmem((size * tok_rows, HEAD_DIM), jnp.bfloat16),
            vmem((size * tok_rows, HEAD_DIM), jnp.bfloat16),
            vmem((2, 2, size * half, HEAD_DIM), jnp.bfloat16),
            vmem((2, 2, size * half, HEAD_DIM), jnp.bfloat16),
            vmem((2, 2, slabs, 2, HEAD_DIM), jnp.float32),
            vmem((2, tok_rows, columns), jnp.bfloat16),
            vmem((2, 2, head_count, 2, HEAD_DIM), jnp.float32),
            vmem((2, 2 * STAT_ROWS, HEAD_DIM), jnp.float32),
            vmem((2 * tok_rows, HEAD_DIM), jnp.float32),
            vmem((tok_rows, columns), jnp.bfloat16),
            vmem((half, width), jnp.float32),
            vmem((2, chunks, half // 2, chunk), jnp.bfloat16),
            vmem((2, chunks, half // 2, chunk), jnp.bfloat16),
            dma((3,)),
            dma,
            dma,
            dma,
            dma,
            dma,
            dma,
            dma,
            dma,
            dma((2,)),
            dma,
            dma((2, LAYER - 1)),
            dma((2,)),
            dma((2, 3)),
            dma((2,)),
            dma((2, 2)),
            dma,
            dma((2, chunks)),
        ],
        compiler_params=pltpu.CompilerParams(
            collective_id=0, has_side_effects=True, vmem_limit_bytes=52 << 20
        ),
    )(*[pltpu.with_memory_space_constraint(x, pltpu.HBM) for x in (frame_tokens, queries, keys, values, wo)])


def solution(mesh):
    in_specs = (P("ctx", "tp"), P("ctx", "tp"), P("ctx", "tp"), P("tp", None), P())
    out_specs = P(("ctx", "tp"), None)
    return jax.shard_map(
        on_device, mesh=mesh, in_specs=in_specs, out_specs=out_specs, check_vma=False
    )
```

```python
import functools
import math

import jax
import jax.numpy as jnp
from jax import lax
from jax.experimental import pallas as pl
from jax.experimental.pallas import tpu as pltpu
from jax.sharding import PartitionSpec as P

HEAD_DIM = 128
LAYER = 4
NEG = -1e30
MESH = pl.DeviceIdType.MESH
FAR, NEAR = 0, 1
STAT_ROWS = 8


def group_size(n):
    levels = n // LAYER
    return n // 2 if levels % 2 == 0 else n


def host_places(size, head_count):
    top = size - LAYER
    order = [top + i for i in (0, 2, 1, 3)] + [0, 2] + [i for i in range(top) if i not in (0, 2)]
    return order[:head_count]


def kernel(
    n,
    chunk,
    counts_hbm,
    q_hbm,
    k_hbm,
    v_hbm,
    wo_hbm,
    out_ref,
    counts_ref,
    q_ref,
    k_pal,
    v_pal,
    wo_all,
    k_in,
    v_in,
    q_in,
    acc_out,
    stat_out,
    acc_in,
    stat_in,
    stat_rows,
    near_stat,
    attended,
    kept,
    outgoing,
    incoming,
    counts_sem,
    in_sem,
    wo_sem,
    k_send,
    v_send,
    q_send,
    far_send,
    k_recv,
    v_recv,
    q_recv,
    far_recv,
    pal_send,
    pal_recv,
    acc_send,
    acc_recv,
    stat_send,
    stat_recv,
    x_send_sem,
    x_recv_sem,
):
    tok_rows, columns = k_hbm.shape
    head_count = columns // HEAD_DIM
    width = wo_hbm.shape[1]
    half = tok_rows // 2
    quarter = half // 2
    chunks = width // chunk
    parts = [(0, quarter), (quarter, quarter), (half, half)]
    me = lax.axis_index("ctx")
    tp = lax.axis_index("tp")
    size = group_size(n)
    split = size < n
    upper = me // size
    base = upper * size
    local = me - base
    is_upper = upper > 0
    is_lower = jnp.logical_not(is_upper)
    is_base = local < LAYER
    is_top = jnp.logical_not(is_base)
    lane = lax.rem(me, LAYER)
    places = host_places(size, head_count)
    my_head = jnp.int32(0)
    is_host = local < 0
    for h, place in enumerate(places):
        my_head = jnp.where(local == place, h, my_head)
        is_host = jnp.logical_or(is_host, local == place)
    my_cols = pl.ds(pl.multiple_of(my_head * HEAD_DIM, HEAD_DIM), HEAD_DIM)
    head_cols = [slice(h * HEAD_DIM, (h + 1) * HEAD_DIM) for h in range(head_count)]
    scale = math.log2(math.e) / math.sqrt(HEAD_DIM)

    def both(a, b):
        return jnp.logical_and(a, b)

    def start_of(b):
        return pl.multiple_of((1 - tp if b == 0 else tp) * half, half)

    def rows_of(src, rows):
        return pl.ds(pl.multiple_of(src * rows, rows), rows)

    pltpu.make_async_copy(k_hbm, k_pal.at[lane], in_sem.at[0]).start()
    pltpu.make_async_copy(v_hbm, v_pal.at[lane], in_sem.at[1]).start()
    for b in range(2):
        pltpu.make_async_copy(q_hbm.at[pl.ds(start_of(b), half), :], q_ref.at[b], in_sem.at[2]).start()

    counts_copy = pltpu.make_async_copy(counts_hbm, counts_ref, counts_sem)
    counts_copy.start()
    wo_copy = pltpu.make_async_copy(wo_hbm, wo_all, wo_sem)
    first_pair = both(both(is_base, is_lower), lane < 2)
    pl.when(first_pair)(wo_copy.start)
    barrier = pltpu.get_barrier_semaphore()

    def greet(dev, other_tp):
        pl.semaphore_signal(barrier, inc=1, device_id=(dev, other_tp), device_id_type=MESH)

    def each(count, body):
        if count <= 16:
            for j in range(count):
                body(j)
        else:
            lax.fori_loop(0, count, lambda j, carry: (body(j), carry)[1], 0)

    greet(me, 1 - tp)
    takes = {1: (0,), 2: (0, 3), 3: (1, 2)}
    for to, sources in takes.items():

        @pl.when(both(is_base, lane == to))
        def _():
            for source in sources:
                greet(base + source, tp)

    @pl.when(is_host)
    def _():
        def other(j):
            @pl.when(local != j)
            def _():
                greet(base + j, tp)

        each(size, other)
        if split:

            @pl.when(is_lower)
            def _():
                each(size, lambda j: greet(size + j, tp))

    gifts = jnp.where(lane == 0, 2, 1)
    expected = 1 + head_count - is_host.astype(jnp.int32) + jnp.where(is_base, gifts, 0)
    if split:
        expected = expected + jnp.where(is_upper, head_count, 0)
    with jax.named_scope("bar"):
        pl.semaphore_wait(barrier, expected)

    def remote(src, dst, send, recv, dev):
        return pltpu.make_async_remote_copy(
            src_ref=src,
            dst_ref=dst,
            send_sem=send,
            recv_sem=recv,
            device_id=(dev, tp),
            device_id_type=MESH,
        )

    def arrived(ref, sem):
        pltpu.make_async_copy(ref, ref, sem).wait()

    def give_k(h, dev):
        return remote(k_pal.at[lane, :, head_cols[h]], k_in.at[rows_of(local, tok_rows)], k_send, k_recv, dev)

    def give_v(h, dev):
        return remote(v_pal.at[lane, :, head_cols[h]], v_in.at[rows_of(local, tok_rows)], v_send, v_recv, dev)

    def give_q(h, dev):
        return remote(q_ref.at[:, :, head_cols[h]], q_in.at[NEAR, :, rows_of(local, half)], q_send, q_recv, dev)

    def give_far(h, b):
        return remote(
            q_ref.at[b, :, head_cols[h]],
            q_in.at[FAR, b, rows_of(local, half)],
            far_send,
            far_recv.at[b],
            places[h],
        )

    def pal(kind, frame, to):
        ref = (k_pal, v_pal)[kind].at[frame]
        return remote(ref, ref, pal_send, pal_recv.at[kind, frame], base + to)

    with jax.named_scope("own"):
        arrived(k_pal.at[lane], in_sem.at[0])
        arrived(v_pal.at[lane], in_sem.at[1])
        arrived(q_ref, in_sem.at[2])
        counts_copy.wait()

    def to_hosts(give):
        for h in nearest_last:
            place = places[h]

            @pl.when(local != place)
            def _():
                give(h, base + place).start()

    nearest_last = sorted(range(head_count), key=lambda h: places[h])

    def to_far(b, who):
        if split:

            @pl.when(both(is_upper, who))
            def _():
                for h in nearest_last:
                    give_far(h, b).start()

    @pl.when(is_host)
    def _():
        pltpu.make_async_copy(k_pal.at[lane, :, my_cols], k_in.at[rows_of(local, tok_rows)], k_recv).start()
        pltpu.make_async_copy(v_pal.at[lane, :, my_cols], v_in.at[rows_of(local, tok_rows)], v_recv).start()

        @pl.when(is_top)
        def _():
            pltpu.make_async_copy(
                q_ref.at[:, :, my_cols], q_in.at[NEAR, :, rows_of(local, half)], q_recv
            ).start()

    @pl.when(both(is_base, lane == 0))
    def _():
        for kind in range(2):
            pal(kind, 0, 1).start()

    @pl.when(both(is_base, lane == 2))
    def _():
        for kind in range(2):
            pal(kind, 2, 3).start()

    to_far(0, is_upper)
    to_far(1, is_base)
    to_hosts(give_k)

    @pl.when(both(is_upper, is_top))
    def _():
        to_hosts(give_q)

    to_hosts(give_v)
    to_far(1, is_top)

    @pl.when(both(is_lower, is_top))
    def _():
        to_hosts(give_q)

    for kind in range(2):
        for source in range(2):

            @pl.when(both(is_base, lane == source))
            def _():
                pal(kind, source, source + 2).start()

    pl.when(jnp.logical_not(first_pair))(wo_copy.start)

    def masked_weights(scores, allowed):
        scores = jnp.where(allowed, scores, NEG)
        top = jnp.max(scores, axis=-1, keepdims=True)
        return top, jnp.exp2((scores - top) * scale).astype(jnp.bfloat16)

    def attend_level():
        col = lax.broadcasted_iota(jnp.int32, (1, LAYER * tok_rows), 1)
        slot = col // tok_rows
        limit = jnp.zeros(col.shape, jnp.int32)
        for f in range(LAYER):
            limit = jnp.where(slot == f, jnp.where(f <= lane, counts_ref[base + f], 0), limit)
        allowed = lax.rem(col, tok_rows) < limit
        ones = jnp.ones((LAYER * tok_rows, HEAD_DIM), jnp.bfloat16)
        frames = [jnp.minimum(f, lane) for f in range(LAYER)]
        at = lax.broadcasted_iota(jnp.int32, (tok_rows, HEAD_DIM), 1)
        begun = []
        for cols in head_cols:
            query = jnp.concatenate([q_ref[0, :, cols], q_ref[1, :, cols]], axis=0)
            keys = jnp.concatenate([k_pal[f, :, cols] for f in frames], axis=0)
            scores = lax.dot_general(
                query, keys, (((1,), (1,)), ((), ())), preferred_element_type=jnp.float32
            )
            begun.append(masked_weights(scores, allowed))
        stats = jnp.zeros((tok_rows, HEAD_DIM), jnp.float32)
        for h, cols in enumerate(head_cols):
            top, weights = begun[h]
            vals = jnp.concatenate([v_pal[f, :, cols] for f in frames], axis=0)
            acc = jnp.dot(weights, jnp.concatenate([vals, ones], axis=1), preferred_element_type=jnp.float32)
            acc_in[NEAR, :, cols] = acc[:, :HEAD_DIM].astype(jnp.bfloat16)
            stats = jnp.where(at == h, top, stats)
            stats = jnp.where(at == STAT_ROWS + h, acc[:, HEAD_DIM:], stats)
        near_stat[:tok_rows, :] = stats

    far_frames = min(size, 256 // half)
    near_frames = min(size - LAYER, HEAD_DIM // half)
    slab_frames = HEAD_DIM // half
    span_frames = min(size, 8)
    span = span_frames * tok_rows
    key_tiles = size // span_frames
    col = lax.broadcasted_iota(jnp.int32, (1, span), 1)
    slot = col // tok_rows
    place_in = lax.rem(col, tok_rows)
    ones = jnp.ones((span, HEAD_DIM), jnp.bfloat16)

    def keys_at(kt):
        return rows_of(kt, span) if key_tiles > 1 else slice(0, span)

    def weigh(query, row_frame, kt, old_max):
        scores = lax.dot_general(
            query, k_in[keys_at(kt), :], (((1,), (1,)), ((), ())), preferred_element_type=jnp.float32
        )
        limit = jnp.zeros((1, span), jnp.int32)
        for f in range(span_frames):
            limit = jnp.where(slot == f, counts_ref[base + kt * span_frames + f], limit)
        allowed = place_in < limit
        if row_frame is not None:
            allowed = jnp.logical_and(allowed, slot + kt * span_frames <= row_frame)
        scores = jnp.where(allowed, scores, NEG)
        top = jnp.max(scores, axis=-1, keepdims=True)
        if old_max is not None:
            top = jnp.maximum(top, old_max)
        return top, jnp.exp2((scores - top) * scale).astype(jnp.bfloat16)

    def gather(weights, kt):
        return jnp.dot(
            weights,
            jnp.concatenate([v_in[keys_at(kt), :], ones], axis=1),
            preferred_element_type=jnp.float32,
        )

    def more_keys(query, row_frame, top, acc):
        if key_tiles == 1:
            return top, acc

        def more(kt, carry):
            old_max, acc = carry
            top, weights = weigh(query, row_frame, kt, old_max)
            return top, jnp.exp2((old_max - top) * scale) * acc + gather(weights, kt)

        return lax.fori_loop(1, key_tiles, more, (top, acc))

    def begin(query, row_frame):
        return query, row_frame, weigh(query, row_frame, 0, None)

    def end(begun):
        query, row_frame, (top, weights) = begun
        return more_keys(query, row_frame, top, gather(weights, 0))

    def acc_copies(kind, p, j, dev):
        first, rows = parts[p]
        b = first // half
        src = acc_out.at[kind, b, pl.ds(j * half + first - b * half, rows)]
        dst = acc_in.at[kind, pl.ds(first, rows), my_cols]
        return src, dst, acc_send.at[kind], acc_recv.at[kind, p], dev

    def stat_copies(kind, b, j, dev):
        return (
            stat_out.at[kind, b, j // slab_frames],
            stat_in.at[kind, b, my_head],
            stat_send.at[kind],
            stat_recv.at[kind, b],
            dev,
        )

    def post(kind, copy, frames):
        for j in frames:
            if kind == FAR:
                remote(*copy(j, size + j)).start()
            else:
                src, dst, send, recv, dev = copy(j, base + j)

                @pl.when(local != j)
                def _():
                    remote(src, dst, send, recv, dev).start()

                @pl.when(local == j)
                def _():
                    pltpu.make_async_copy(src, dst, recv).start()

    def stats_from(kind, b, first, top, acc):
        at = lax.broadcasted_iota(jnp.int32, acc[:, HEAD_DIM:].shape, 1)
        stats = jnp.where(at == 0, top, acc[:, HEAD_DIM:])
        for s in range(stats.shape[0] // HEAD_DIM):
            turned = jnp.transpose(stats[s * HEAD_DIM : (s + 1) * HEAD_DIM])
            stat_out[kind, b, first // slab_frames + s] = turned[:2]

    def begin_far(b, t):
        return begin(q_in[FAR, b, t * far_frames * half : (t + 1) * far_frames * half, :], None)

    def serve_far(b, t, begun):
        top, acc = end(begun)
        first = t * far_frames
        acc_out[FAR, b, first * half : (first + far_frames) * half, :] = acc[:, :HEAD_DIM].astype(jnp.bfloat16)
        frames = sorted(range(first, first + far_frames), key=lambda j: (j % LAYER >= LAYER // 2, -j))
        mine = [p for p, (at, rows) in enumerate(parts) if at // half == b]
        post(FAR, lambda j, dev: acc_copies(FAR, mine[0], j, dev), frames)
        stats_from(FAR, b, first, top, acc)
        post(FAR, lambda j, dev: stat_copies(FAR, b, j, dev), frames)
        for p in mine[1:]:
            post(FAR, lambda j, dev: acc_copies(FAR, p, j, dev), frames)

    near_rows = near_frames * half
    near_tiles = (size - LAYER) // near_frames

    def near_at(t):
        first = LAYER + t * near_frames
        return first, slice(first * half, (first + near_frames) * half)

    def begin_near(t):
        first, at = near_at(t)
        row = lax.broadcasted_iota(jnp.int32, (2 * near_rows, 1), 0)
        query = jnp.concatenate([q_in[NEAR, 0, at, :], q_in[NEAR, 1, at, :]], axis=0)
        return begin(query, first + lax.rem(row, near_rows) // half)

    def serve_near(t, begun):
        top, acc = end(begun)
        first, at = near_at(t)
        for b in range(2):
            rows = slice(b * near_rows, (b + 1) * near_rows)
            acc_out[NEAR, b, at, :] = acc[rows, :HEAD_DIM].astype(jnp.bfloat16)
        frames = range(first + near_frames - 1, first - 1, -1)
        post(NEAR, lambda j, dev: acc_copies(NEAR, 0, j, dev), frames)
        for b in range(2):
            rows = slice(b * near_rows, (b + 1) * near_rows)
            stats_from(NEAR, b, first, top[rows], acc[rows])
            post(NEAR, lambda j, dev: stat_copies(NEAR, b, j, dev), frames)
        for p in (1, 2):
            post(NEAR, lambda j, dev: acc_copies(NEAR, p, j, dev), frames)

    def serve_all_near(begun):
        with jax.named_scope("sn"):
            for t in range(near_tiles):
                serve_near(t, begun if begun is not None else begin_near(t))

    def serve_all_far(b, begun):
        with jax.named_scope("sf"):
            for t in range(size // far_frames):
                serve_far(b, t, begun if begun is not None else begin_far(b, t))

    def host():
        with jax.named_scope("wk"):
            arrived(k_in, k_recv)

        def wait_near():
            with jax.named_scope("wq"):
                arrived(q_in.at[NEAR, :, LAYER * half :], q_recv)

        def host_near():
            wait_near()
            with jax.named_scope("bn"):
                begun = begin_near(0) if near_tiles == 1 and key_tiles == 1 else None
            with jax.named_scope("wv"):
                arrived(v_in, v_recv)
            serve_all_near(begun)

        def wait_far(b):
            with jax.named_scope("wf"):
                arrived(q_in.at[FAR, b], far_recv.at[b])

        def host_both():
            @pl.when(is_top)
            def _():
                wait_far(0)
                with jax.named_scope("bf"):
                    begun = begin_far(0, 0) if size == far_frames and key_tiles == 1 else None
                with jax.named_scope("wv"):
                    arrived(v_in, v_recv)
                serve_all_far(0, begun)
                wait_near()
                serve_all_near(None)

            @pl.when(is_base)
            def _():
                host_near()
                wait_far(0)
                serve_all_far(0, None)

            wait_far(1)
            serve_all_far(1, None)

        if split:
            pl.when(is_lower)(host_both)
            pl.when(is_upper)(host_near)
        else:
            host_near()

    lead = lax.rem(local, slab_frames) * half
    row = lax.broadcasted_iota(jnp.int32, (half, HEAD_DIM), 0)
    padding = jnp.zeros((HEAD_DIM - 2 * STAT_ROWS, HEAD_DIM), jnp.float32)

    def stat_columns(kind, b):
        for h in range(head_count):
            stat_rows[kind, h : h + 1, :] = stat_in[kind, b, h, 0:1, :]
            stat_rows[kind, STAT_ROWS + h : STAT_ROWS + h + 1, :] = stat_in[kind, b, h, 1:2, :]
        turned = jnp.transpose(jnp.concatenate([stat_rows[kind], padding], axis=0))
        picked = turned[:half]
        for i in range(1, slab_frames):
            picked = jnp.where(lead == i * half, turned[i * half : (i + 1) * half], picked)
        return picked

    def sums(stats):
        return pltpu.roll(stats, HEAD_DIM - STAT_ROWS, 1)

    def swap(p, c):
        first, rows = parts[p]
        return pltpu.make_async_remote_copy(
            src_ref=outgoing.at[p, c],
            dst_ref=incoming.at[p, c],
            send_sem=x_send_sem,
            recv_sem=x_recv_sem.at[p, c],
            device_id=(me, 1 - tp),
            device_id_type=MESH,
        )

    def own_rows(which, from_hosts, from_far):
        for p in which:
            first, rows = parts[p]
            b = first // half
            if from_hosts:

                @pl.when(is_top)
                def _():
                    with jax.named_scope("wan"):
                        arrived(acc_in.at[NEAR, pl.ds(first, rows)], acc_recv.at[NEAR, p])
                        if first % half == 0:
                            arrived(stat_in.at[NEAR, b], stat_recv.at[NEAR, b])
                            near_stat[b * half : (b + 1) * half, :] = stat_columns(NEAR, b)

            live = row[:rows] + (start_of(b) + first - b * half) < counts_ref[me]

            def merge(far):
                near = near_stat[first : first + rows, :]
                if far:
                    other = near_stat[tok_rows + first : tok_rows + first + rows, :]
                    top = jnp.maximum(near, other)
                    near_part = jnp.exp2((near - top) * scale)
                    far_part = jnp.exp2((other - top) * scale)
                    total = near_part * sums(near) + far_part * sums(other)
                    factors = ((NEAR, near_part / total), (FAR, far_part / total))
                else:
                    factors = ((NEAR, 1.0 / sums(near)),)
                for h, cols in enumerate(head_cols):
                    out = 0.0
                    for kind, factor in factors:
                        out = out + factor[:, h : h + 1] * acc_in[kind, first : first + rows, cols].astype(
                            jnp.float32
                        )
                    attended[first : first + rows, cols] = jnp.where(live, out, 0.0).astype(jnp.bfloat16)

            if from_far:

                @pl.when(is_upper)
                def _():
                    with jax.named_scope("waf"):
                        arrived(acc_in.at[FAR, pl.ds(first, rows)], acc_recv.at[FAR, p])
                        if first % half == 0:
                            arrived(stat_in.at[FAR, b], stat_recv.at[FAR, b])
                            near_stat[tok_rows + b * half : tok_rows + (b + 1) * half, :] = stat_columns(FAR, b)
                    merge(True)

                @pl.when(is_lower)
                def _():
                    merge(False)

            else:
                merge(False)

            if p == 0:
                wo_copy.wait()
            with jax.named_scope("proj"):
                lhs = attended[first : first + rows, :]
                for c in range(chunks):
                    part = jnp.dot(
                        lhs, wo_all[:, c * chunk : (c + 1) * chunk], preferred_element_type=jnp.float32
                    )
                    if b == 0:
                        outgoing[p, c] = part.astype(jnp.bfloat16)
                        swap(p, c).start()
                    else:
                        kept[:, c * chunk : (c + 1) * chunk] = part

    def pass_on(frame, to):
        for kind in range(2):
            arrived((k_pal, v_pal)[kind].at[frame], pal_recv.at[kind, frame])
            if to is not None:
                pal(kind, frame, to).start()

    @pl.when(both(is_base, lane < 2))
    def _():
        with jax.named_scope("pal"):

            @pl.when(lane == 1)
            def _():
                pass_on(0, None)

        with jax.named_scope("lev"):
            attend_level()

        @pl.when(is_lower)
        def _():
            own_rows((0,), False, False)

    pl.when(is_host)(host)

    @pl.when(both(is_base, lane >= 2))
    def _():
        with jax.named_scope("pal"):

            @pl.when(lane == 2)
            def _():
                pass_on(0, 3)
                pass_on(1, None)

            @pl.when(lane == 3)
            def _():
                pass_on(1, 2)
                pass_on(2, None)
                pass_on(0, None)

        with jax.named_scope("lev"):
            attend_level()

        @pl.when(is_lower)
        def _():
            own_rows((0,), False, False)

    @pl.when(both(is_base, is_lower))
    def _():
        own_rows((1, 2), False, False)

    @pl.when(jnp.logical_not(both(is_base, is_lower)))
    def _():
        own_rows((0, 1, 2), True, split)

    with jax.named_scope("drain"):

        def given(count):
            arrived(k_pal.at[0, :, : count * HEAD_DIM], k_send)
            arrived(v_pal.at[0, :, : count * HEAD_DIM], v_send)

            @pl.when(is_top)
            def _():
                arrived(q_ref.at[:, :, : count * HEAD_DIM], q_send)

        def answered(kind, count):
            arrived(acc_out.at[kind, :, : count * half], acc_send.at[kind])
            arrived(acc_out.at[kind, :, : count * 4], stat_send.at[kind])

        @pl.when(is_host)
        def _():
            given(head_count - 1)

            @pl.when(is_top)
            def _():
                answered(NEAR, size - LAYER - 1)

            @pl.when(is_base)
            def _():
                answered(NEAR, size - LAYER)

            if split:

                @pl.when(is_lower)
                def _():
                    answered(FAR, size)

        @pl.when(jnp.logical_not(is_host))
        def _():
            given(head_count)

        if split:

            @pl.when(is_upper)
            def _():
                arrived(q_ref, far_send)

        for lanes, count in (((0, 2), 2), ((1, 3), 1)):

            @pl.when(both(is_base, jnp.logical_or(lane == lanes[0], lane == lanes[1])))
            def _():
                arrived(k_pal.at[: 2 * count], pal_send)

    for c in range(chunks):
        at = slice(c * chunk, (c + 1) * chunk)
        for p in range(2):
            first, rows = parts[p]
            with jax.named_scope("swapw"):
                arrived(incoming.at[p, c], x_recv_sem.at[p, c])
            out_ref[first : first + rows, at] = (
                kept[first : first + rows, at] + incoming[p, c].astype(jnp.float32)
            ).astype(out_ref.dtype)
    with jax.named_scope("fin"):
        arrived(outgoing, x_send_sem)


def on_device(queries, keys, values, wo, frame_tokens):
    tok_rows, columns = queries.shape
    width = wo.shape[1]
    n = lax.axis_size("ctx")
    half = tok_rows // 2
    chunk = 512 if width % 512 == 0 else width
    chunks = width // chunk
    head_count = columns // HEAD_DIM
    size = group_size(n)
    slabs = size * half // HEAD_DIM
    vmem = pltpu.VMEM
    dma = pltpu.SemaphoreType.DMA
    return pl.pallas_call(
        functools.partial(kernel, n, chunk),
        out_shape=jax.ShapeDtypeStruct((half, width), jnp.bfloat16),
        in_specs=[
            pl.BlockSpec(memory_space=pltpu.HBM),
            pl.BlockSpec(memory_space=pltpu.HBM),
            pl.BlockSpec(memory_space=pltpu.HBM),
            pl.BlockSpec(memory_space=pltpu.HBM),
            pl.BlockSpec(memory_space=pltpu.HBM),
        ],
        out_specs=pl.BlockSpec(memory_space=vmem),
        scratch_shapes=[
            pltpu.SMEM((n,), jnp.int32),
            vmem((2, half, columns), jnp.bfloat16),
            vmem((LAYER, tok_rows, columns), jnp.bfloat16),
            vmem((LAYER, tok_rows, columns), jnp.bfloat16),
            vmem(wo.shape, jnp.bfloat16),
            vmem((size * tok_rows, HEAD_DIM), jnp.bfloat16),
            vmem((size * tok_rows, HEAD_DIM), jnp.bfloat16),
            vmem((2, 2, size * half, HEAD_DIM), jnp.bfloat16),
            vmem((2, 2, size * half, HEAD_DIM), jnp.bfloat16),
            vmem((2, 2, slabs, 2, HEAD_DIM), jnp.float32),
            vmem((2, tok_rows, columns), jnp.bfloat16),
            vmem((2, 2, head_count, 2, HEAD_DIM), jnp.float32),
            vmem((2, 2 * STAT_ROWS, HEAD_DIM), jnp.float32),
            vmem((2 * tok_rows, HEAD_DIM), jnp.float32),
            vmem((tok_rows, columns), jnp.bfloat16),
            vmem((half, width), jnp.float32),
            vmem((2, chunks, half // 2, chunk), jnp.bfloat16),
            vmem((2, chunks, half // 2, chunk), jnp.bfloat16),
            dma,
            dma((3,)),
            dma,
            dma,
            dma,
            dma,
            dma,
            dma,
            dma,
            dma,
            dma((2,)),
            dma,
            dma((2, LAYER - 1)),
            dma((2,)),
            dma((2, 3)),
            dma((2,)),
            dma((2, 2)),
            dma,
            dma((2, chunks)),
        ],
        compiler_params=pltpu.CompilerParams(
            collective_id=0, has_side_effects=True, vmem_limit_bytes=52 << 20
        ),
    )(*[pltpu.with_memory_space_constraint(x, pltpu.HBM) for x in (frame_tokens, queries, keys, values, wo)])


def solution(mesh):
    in_specs = (P("ctx", "tp"), P("ctx", "tp"), P("ctx", "tp"), P("tp", None), P())
    out_specs = P(("ctx", "tp"), None)
    return jax.shard_map(
        on_device, mesh=mesh, in_specs=in_specs, out_specs=out_specs, check_vma=False
    )
```
